512 devices in a mesh: ctx: 64 (over z_lo, y, core), head: 8 (over z_hi, x).
Axes of the slice: x: 4, y: 4, z: 16 (z_hi: 2, z_lo: 8; z = z_hi * 8 + z_lo), core: 2. Of those that a mesh axis runs over, the one named last changes fastest.
Arguments:
- queries: bfloat16 [8192, 4096], P('ctx', 'head'), may hold values from -8 to 8
- keys: bfloat16 [8192, 1024], P('ctx', 'head'), may hold values from -6 to 6
- values: bfloat16 [8192, 1024], P('ctx', 'head'), may hold values from -6 to 6
- out_weight: bfloat16 [4096, 8192], P('head', 'ctx'), may hold values from -2.390625 to 2.390625
- block_order: int32 [128], replicated, may hold values from 0 to 127, as said below
Outputs:
- projected: bfloat16 [8192, 8192], P('ctx', 'head')
The draws below stay inside these ranges and needn't reach their ends.
Inputs may be any that keep to these rules, and one draw needn't show every extreme that they name: `block_order`: slot blocks 2 s and 2 s + 1 hold the position blocks p and 127 - p for some p, and each position block is held by exactly one slot block.
All inputs are finite; a program needn't handle non-finite values.
Results may differ from the reference program's by a relative error of at most 0.018.
Values may be sent and summed in bfloat16 or wider, within the bound.
No kernel may reach another device: no remote copies, remote signals or barrier semaphores. Data moves between devices by JAX's collectives and lax.ppermute only.
A program may use at most 128 MiB of HBM per device.

```python
import math
import jax
import jax.numpy as jnp
from jax import lax

D = 8192
DH = 128
HQ_DEV = 4
GROUPS = 8
HEADS = 32
SEQ = 8192
BLOCK = 64
N_CTX = 64


def draw_queries(key, part):
    first = jax.random.fold_in(key, 0)
    return jnp.clip(2.0 * jax.random.normal(first, (SEQ, HEADS * DH), jnp.float32), -8.0, 8.0).astype(jnp.bfloat16)


def draw_keys(key, part):
    first = jax.random.fold_in(jax.random.fold_in(key, 11), 0)
    return jnp.clip(jax.random.normal(first, (SEQ, GROUPS * DH), jnp.float32), -6.0, 6.0).astype(jnp.bfloat16)


def draw_block_order(key, part):
    order = jax.random.permutation(jax.random.fold_in(key, 23), N_CTX).astype(jnp.int32)
    mirror = (2 * N_CTX - 1 - order).astype(jnp.int32)
    return jnp.stack([order, mirror], axis=1).reshape(2 * N_CTX).astype(jnp.int32)


def shard_levels(rng, extent, cuts, least, top_value):
    def one(dim, parts):
        steps = jax.random.uniform(jax.random.fold_in(jax.random.fold_in(rng, 6), dim), (parts,), jnp.float32, least / len(cuts), top_value / len(cuts))
        return jnp.repeat(jnp.exp(steps), extent[dim] // parts).reshape((-1,) + (1,) * (len(extent) - dim - 1))

    factor_of = one(*cuts[0])
    for cut in cuts[1:]:
        factor_of = factor_of * one(*cut)
    return factor_of


def normal_values(rng, shape, deviation, bound, cuts=(), kind=jnp.bfloat16):
    entries = deviation * jax.random.normal(rng, shape, jnp.float32)
    if cuts:
        entries = entries * shard_levels(rng, shape, cuts, -0.22, 0.18)
    return jnp.clip(entries, -bound, bound).astype(kind)


def setup_inputs(seed: int = 0) -> dict:
    key_list = jax.random.split(jax.random.key(seed), 6)
    return {
        "queries": draw_queries(jax.random.fold_in(key_list[5], 71), 0),
        "keys": draw_keys(jax.random.fold_in(key_list[5], 71), 0),
        "values": normal_values(key_list[2], (SEQ, GROUPS * DH), 1.0, 6.0, ((0, 64), (1, 8))),
        "out_weight": normal_values(key_list[3], (HEADS * DH, D), 0.3, 2.390625, ((0, 8), (1, 64))),
        "block_order": draw_block_order(jax.random.fold_in(key_list[5], 71), 0),
    }


def slot_positions(block_order):
    row_index = jnp.arange(SEQ, dtype=jnp.int32)
    return (block_order[row_index // BLOCK] * BLOCK + row_index % BLOCK).astype(jnp.int32)

def reference(queries, keys, values, out_weight, block_order):
    position = slot_positions(block_order)
    scaling = 1.0 / math.sqrt(DH)
    query_block = min(512, SEQ)
    blocks = SEQ // query_block
    grouped_pos = position.reshape(blocks, query_block)
    query_groups = jnp.transpose(queries.reshape(SEQ, GROUPS, HQ_DEV, DH), (1, 0, 2, 3))
    key_groups = jnp.transpose(keys.reshape(SEQ, GROUPS, DH), (1, 0, 2))
    value_groups = jnp.transpose(values.reshape(SEQ, GROUPS, DH), (1, 0, 2))

    def attend_group(inputs):
        group_queries, group_keys, group_values = inputs
        keys_wide = group_keys.astype(jnp.float32)
        values_wide = group_values.astype(jnp.float32)
        split_queries = group_queries.reshape(blocks, query_block, HQ_DEV, DH)

        def attend_block(pieces):
            query_part, query_pos = pieces
            scores = jnp.einsum('thd,sd->hts', query_part.astype(jnp.float32), keys_wide) * scaling
            visible = position[None, None, :] <= query_pos[None, :, None]
            scores = jnp.where(visible, scores, -1e+30)
            largest = lax.optimization_barrier(jnp.max(scores, axis=-1, keepdims=True))
            weights = jnp.where(visible, jnp.exp(scores - largest), 0.0)
            denominator = lax.optimization_barrier(jnp.sum(weights, axis=-1))
            weights_b = weights.astype(jnp.bfloat16)
            summed = jnp.einsum('hts,sd->htd', weights_b.astype(jnp.float32), values_wide)
            return (summed / denominator[..., None]).astype(jnp.bfloat16)
        return lax.map(attend_block, (split_queries, grouped_pos))
    attended = lax.map(attend_group, (query_groups, key_groups, value_groups))
    attended = jnp.transpose(attended, (0, 2, 1, 3, 4)).reshape(HEADS, SEQ, DH)
    weight_heads = out_weight.reshape(HEADS, DH, D)

    def add_head(carry, inputs):
        head_rows, head_weight = inputs
        partial_value = jnp.dot(head_rows, head_weight, preferred_element_type=jnp.float32).astype(jnp.bfloat16)
        partial_value = lax.optimization_barrier(partial_value)
        return (carry + partial_value.astype(jnp.float32), None)
    summed, _ = lax.scan(add_head, jnp.zeros((SEQ, D), jnp.float32), (attended, weight_heads))
    return summed.astype(jnp.bfloat16)
```

```python
import math

import jax
import jax.numpy as jnp
from jax import lax
from jax.experimental import pallas as pl
from jax.experimental.pallas import tpu as pltpu
from jax.sharding import Mesh
from jax.sharding import PartitionSpec as P

AXES = ("za", "zb", "y", "c", "h", "x")
SIZES = (2, 4, 4, 2, 2, 4)
CTX = ("za", "zb", "y", "c")
HEAD = ("h", "x")
DH = 128
TOK = 128
HEADS = 4
FEAT = HEADS * DH
STATS = 16
NEG = -1e30
F32 = jnp.float32
BF16 = jnp.bfloat16


def swap(value, axis, size, bit):
    return lax.ppermute(value, axis, [(i, i ^ bit) for i in range(size)])


def attend_kernel(where, order, q_ref, near_ref, far_ref, out_ref, score, prob, v_t, stat):
    za, zb, y, c = where[0], where[1], where[2], where[3]
    scale = math.log2(math.e) / math.sqrt(DH)
    lane = lax.broadcasted_iota(jnp.int32, (1, TOK), 1)
    half = lane // 64

    def slot(ctx, index, which):
        return jnp.where(which == 0, order[2 * ctx], order[2 * ctx + 1]) * 64 + index % 64

    base = (za * 4 + zb) * 4
    q_pos = jnp.concatenate([slot((base + j) * 2 + c, lane, half) for j in range(4)], axis=1)
    row = lax.broadcasted_iota(jnp.int32, (TOK, 1), 0)
    k_pos = []
    for side, ref in enumerate((near_ref, far_ref)):
        for p in range(8):
            a = za ^ (p & 1)
            b = zb ^ ((p >> 1) & 1) * 2 ^ ((p >> 2) & 1)
            ctx = ((a * 4 + b) * 4 + y) * 2 + (c ^ side)
            k_pos.append(slot(ctx, row, row // 64))
            v_t[:, (side * 8 + p) * TOK : (side * 8 + p + 1) * TOK] = ref[p, TOK:, :].T
    stat[...] = jnp.zeros_like(stat)
    for h in range(HEADS):
        q = jnp.concatenate([q_ref[j, :, h * DH : (h + 1) * DH] for j in range(4)], axis=0)
        top = jnp.full((1, 4 * TOK), NEG, F32)
        for p in range(16):
            k = (near_ref if p < 8 else far_ref)[p % 8, :TOK, :]
            s = lax.dot_general(k, q, (((1,), (1,)), ((), ())), preferred_element_type=F32)
            s = jnp.where(k_pos[p] <= q_pos, s * scale, NEG)
            score[p * TOK : (p + 1) * TOK, :] = s
            top = jnp.maximum(top, jnp.max(s, axis=0, keepdims=True))
        total = jnp.zeros((1, 4 * TOK), F32)
        for p in range(16):
            e = jnp.exp2(score[p * TOK : (p + 1) * TOK, :] - top)
            total = total + jnp.sum(e, axis=0, keepdims=True)
            prob[p * TOK : (p + 1) * TOK, :] = e.astype(BF16)
        o = jnp.dot(v_t[...], prob[...], preferred_element_type=F32) / total
        for j in range(4):
            out_ref[j, h * DH : (h + 1) * DH, :] = o[:, j * TOK : (j + 1) * TOK].astype(BF16)
        rest = top + jnp.log2(total)
        for i in range(3):
            part = rest.astype(BF16).astype(F32)
            stat[3 * h + i : 3 * h + i + 1, :] = part
            rest = rest - part
    for j in range(4):
        out_ref[j, FEAT:, :] = stat[:, j * TOK : (j + 1) * TOK].astype(BF16)


def merge_kernel(in_ref, out_ref):
    stats = [in_ref[j, FEAT:, :].astype(F32) for j in range(4)]
    for h in range(HEADS):
        logs = [s[3 * h : 3 * h + 1] + s[3 * h + 1 : 3 * h + 2] + s[3 * h + 2 : 3 * h + 3] for s in stats]
        top = jnp.maximum(jnp.maximum(logs[0], logs[1]), jnp.maximum(logs[2], logs[3]))
        parts = [jnp.exp2(s - top) for s in logs]
        total = parts[0] + parts[1] + parts[2] + parts[3]
        o = jnp.zeros((DH, TOK), F32)
        for j in range(4):
            o = o + in_ref[j, h * DH : (h + 1) * DH, :].astype(F32) * (parts[j] / total)
        out_ref[:, h * DH : (h + 1) * DH] = o.T.astype(BF16)


def project_kernel(where, a_ref, near_ref, far_ref, out_ref):
    za, zb, c, h = where[0], where[1], where[3], where[4]
    for r in range(4):
        dest = zb ^ (r & 1) * 2 ^ ((r >> 1) & 1)
        w = []
        for g in range(2):
            near, far = near_ref[2 * r + g], far_ref[2 * r + g]
            left = jnp.where(c == 0, near, far)
            right = jnp.where(c == 0, far, near)
            w.append(jnp.concatenate([left, right], axis=1))
        for j in range(4):
            acc = jnp.zeros((TOK, 2 * TOK), F32)
            for g in range(2):
                a = a_ref[j, za ^ g ^ h]
                acc = acc + jnp.dot(a, w[g], preferred_element_type=F32)
            out_ref[dest * 4 + j] = acc.astype(BF16)


def add_kernel(in_ref, out_ref):
    for j in range(4):
        total = in_ref[j].astype(F32)
        for i in range(1, 4):
            total = total + in_ref[i * 4 + j].astype(F32)
        out_ref[:, j * 256 : (j + 1) * 256] = total.astype(BF16)


SM = pl.BlockSpec(memory_space=pltpu.SMEM)
VM = pl.BlockSpec(memory_space=pltpu.VMEM)
PARAMS = pltpu.CompilerParams(vmem_limit_bytes=40 << 20)


def local(queries, keys, values, out_weight, block_order):
    where = jnp.stack([lax.axis_index(a).astype(jnp.int32) for a in AXES])
    kv = jnp.concatenate([keys, values], axis=0)[None]
    z4 = swap(kv, "za", 2, 1)
    q_all = lax.all_to_all(jnp.broadcast_to(queries[None], (4,) + queries.shape), "y", 0, 0, tiled=True)
    kv = jnp.concatenate([kv, z4], axis=0)
    kv = jnp.concatenate([kv, swap(kv, "zb", 4, 2)], axis=0)
    kv = jnp.concatenate([kv, swap(kv, "zb", 4, 1)], axis=0)
    kv, w = lax.optimization_barrier((kv, out_weight))
    kv_far = swap(kv, "c", 2, 1)

    w = lax.ppermute(w, ("za", "h"), [(0, 0), (1, 2), (2, 1), (3, 3)])[None]
    w = jnp.concatenate([w, swap(w, "za", 2, 1)], axis=0)
    w = jnp.concatenate([w, swap(w, "zb", 4, 2)], axis=0)
    w = jnp.concatenate([w, swap(w, "zb", 4, 1)], axis=0)
    w_far = swap(w, "c", 2, 1)

    part = pl.pallas_call(
        attend_kernel,
        out_shape=jax.ShapeDtypeStruct((4, FEAT + STATS, TOK), BF16),
        in_specs=[SM, SM, VM, VM, VM],
        out_specs=VM,
        scratch_shapes=[
            pltpu.VMEM((16 * TOK, 4 * TOK), F32),
            pltpu.VMEM((16 * TOK, 4 * TOK), BF16),
            pltpu.VMEM((DH, 16 * TOK), BF16),
            pltpu.VMEM((STATS, 4 * TOK), F32),
        ],
        compiler_params=PARAMS,
        name="attend",
    )(where, block_order, q_all, kv, kv_far)
    part = lax.all_to_all(part, "y", 0, 0, tiled=True)
    attended = pl.pallas_call(
        merge_kernel,
        out_shape=jax.ShapeDtypeStruct((TOK, FEAT), BF16),
        in_specs=[VM],
        out_specs=VM,
        compiler_params=PARAMS,
        name="merge",
    )(part)
    other = swap(attended, "h", 2, 1)
    pair = jnp.stack([attended, other])
    a_all = lax.all_to_all(jnp.broadcast_to(pair[None], (4,) + pair.shape), "y", 0, 0, tiled=True)
    tiles = pl.pallas_call(
        project_kernel,
        out_shape=jax.ShapeDtypeStruct((16, TOK, 256), BF16),
        in_specs=[SM, VM, VM, VM],
        out_specs=VM,
        compiler_params=PARAMS,
        name="project",
    )(where, a_all, w, w_far)
    tiles = lax.all_to_all(tiles, ("x", "y"), 0, 0, tiled=True)
    return pl.pallas_call(
        add_kernel,
        out_shape=jax.ShapeDtypeStruct((TOK, 1024), BF16),
        in_specs=[VM],
        out_specs=VM,
        compiler_params=PARAMS,
        name="add",
    )(tiles)


def solution(mesh):
    fine = Mesh(mesh.devices.reshape(SIZES), AXES)
    in_specs = (P(CTX, HEAD), P(CTX, HEAD), P(CTX, HEAD), P(HEAD, CTX), P())
    return jax.shard_map(local, mesh=fine, in_specs=in_specs, out_specs=P(CTX, HEAD), check_vma=False)
```

```python
import functools
import math

import jax
import jax.numpy as jnp
from jax import lax
from jax.experimental import pallas as pl
from jax.experimental.pallas import tpu as pltpu
from jax.sharding import Mesh
from jax.sharding import PartitionSpec as P

AXES = ("za", "zb", "y", "c", "h", "x")
SIZES = (2, 4, 4, 2, 2, 4)
CTX = ("za", "zb", "y", "c")
HEAD = ("h", "x")
DH = 128
TOK = 128
HEADS = 4
FEAT = HEADS * DH
STATS = 16
NEG = -1e30
F32 = jnp.float32
BF16 = jnp.bfloat16


def swap(value, axis, size, bit):
    return lax.ppermute(value, axis, [(i, i ^ bit) for i in range(size)])


def attend_kernel(sides, first, last, where, order, *refs):
    q_refs, refs = refs[:4], refs[4:]
    pieces, refs = refs[: len(sides)], refs[len(sides) :]
    if not first:
        acc_in, stat_in, *refs = refs
    if last:
        out_ref, *refs = refs
    else:
        acc_out, stat_out, *refs = refs
    score, prob, v_t, parts = refs
    za, zb, y, c = where[0], where[1], where[2], where[3]
    scale = math.log2(math.e) / math.sqrt(DH)
    lane = lax.broadcasted_iota(jnp.int32, (1, TOK), 1)
    row = lax.broadcasted_iota(jnp.int32, (TOK, 1), 0)

    def slot(ctx, index):
        return jnp.where(index < 64, order[2 * ctx], order[2 * ctx + 1]) * 64 + index % 64

    q_pos = jnp.concatenate([slot(((za * 4 + zb) * 4 + (y ^ j)) * 2 + c, lane) for j in range(4)], axis=1)
    blocks = []
    for ref, (a, side) in zip(pieces, sides):
        for p in range(4):
            n = len(blocks)
            v_t[:, n * TOK : (n + 1) * TOK] = ref[p, TOK:, :].T
            blocks.append((ref, p, slot((((za ^ a) * 4 + p) * 4 + y) * 2 + (c ^ side), row)))
    if last:
        parts[...] = jnp.zeros_like(parts)
    for h in range(HEADS):
        q = jnp.concatenate([ref[:, h * DH : (h + 1) * DH] for ref in q_refs], axis=0)
        top = jnp.full((1, 4 * TOK), NEG, F32) if first else stat_in[h : h + 1, :]
        before = top
        for n, (ref, p, k_pos) in enumerate(blocks):
            s = lax.dot_general(ref[p, :TOK, :], q, (((1,), (1,)), ((), ())), preferred_element_type=F32)
            s = jnp.where(k_pos <= q_pos, s * scale, NEG)
            score[n * TOK : (n + 1) * TOK, :] = s
            top = jnp.maximum(top, jnp.max(s, axis=0, keepdims=True))
        total = jnp.zeros((1, 4 * TOK), F32)
        for n in range(len(blocks)):
            e = jnp.exp2(score[n * TOK : (n + 1) * TOK, :] - top)
            total = total + jnp.sum(e, axis=0, keepdims=True)
            prob[n * TOK : (n + 1) * TOK, :] = e.astype(BF16)
        o = jnp.dot(v_t[...], prob[...], preferred_element_type=F32)
        if not first:
            keep = jnp.exp2(before - top)
            total = total + stat_in[HEADS + h : HEADS + h + 1, :] * keep
            o = o + acc_in[h] * keep
        if not last:
            acc_out[h] = o
            stat_out[h : h + 1, :] = top
            stat_out[HEADS + h : HEADS + h + 1, :] = total
            continue
        o = o / total
        for j in range(4):
            out_ref[y ^ j, h * DH : (h + 1) * DH, :] = o[:, j * TOK : (j + 1) * TOK].astype(BF16)
        rest = top + jnp.log2(total)
        for i in range(3):
            part = rest.astype(BF16).astype(F32)
            parts[3 * h + i : 3 * h + i + 1, :] = part
            rest = rest - part
    if last:
        for j in range(4):
            out_ref[y ^ j, FEAT:, :] = parts[:, j * TOK : (j + 1) * TOK].astype(BF16)


def merge_kernel(in_ref, out_ref):
    stats = [in_ref[j, FEAT:, :].astype(F32) for j in range(4)]
    for h in range(HEADS):
        logs = [s[3 * h : 3 * h + 1] + s[3 * h + 1 : 3 * h + 2] + s[3 * h + 2 : 3 * h + 3] for s in stats]
        top = jnp.maximum(jnp.maximum(logs[0], logs[1]), jnp.maximum(logs[2], logs[3]))
        parts = [jnp.exp2(s - top) for s in logs]
        total = parts[0] + parts[1] + parts[2] + parts[3]
        o = jnp.zeros((DH, TOK), F32)
        for j in range(4):
            o = o + in_ref[j, h * DH : (h + 1) * DH, :].astype(F32) * (parts[j] / total)
        out_ref[:, h * DH : (h + 1) * DH] = o.T.astype(BF16)


def project_kernel(where, own_ref, other_ref, near_ref, far_ref, out_ref):
    za, zb, c, h = where[0], where[1], where[3], where[4]
    for r in range(4):
        dest = zb ^ (r & 1) * 2 ^ ((r >> 1) & 1)
        w = []
        for g in range(2):
            near, far = near_ref[2 * r + g], far_ref[2 * r + g]
            left = jnp.where(c == 0, near, far)
            right = jnp.where(c == 0, far, near)
            w.append(jnp.concatenate([left, right], axis=1))
        w_own = jnp.where(za == h, w[0], w[1])
        w_other = jnp.where(za == h, w[1], w[0])
        for j in range(4):
            acc = jnp.dot(own_ref[j], w_own, preferred_element_type=F32)
            acc = acc + jnp.dot(other_ref[j], w_other, preferred_element_type=F32)
            out_ref[dest * 4 + j] = acc.astype(BF16)


def add_kernel(in_ref, out_ref):
    for j in range(4):
        total = in_ref[j].astype(F32)
        for i in range(1, 4):
            total = total + in_ref[i * 4 + j].astype(F32)
        out_ref[:, j * 256 : (j + 1) * 256] = total.astype(BF16)


SM = pl.BlockSpec(memory_space=pltpu.SMEM)
VM = pl.BlockSpec(memory_space=pltpu.VMEM)
PARAMS = pltpu.CompilerParams(vmem_limit_bytes=40 << 20)


def attend(sides, first, last, where, order, q, *arrays):
    keys = len(sides) * 4 * TOK
    if last:
        out_shape = jax.ShapeDtypeStruct((4, FEAT + STATS, TOK), BF16)
        out_specs = VM
    else:
        out_shape = (
            jax.ShapeDtypeStruct((HEADS, DH, 4 * TOK), F32),
            jax.ShapeDtypeStruct((2 * HEADS, 4 * TOK), F32),
        )
        out_specs = (VM, VM)
    return pl.pallas_call(
        functools.partial(attend_kernel, sides, first, last),
        out_shape=out_shape,
        in_specs=[SM, SM] + [VM] * (4 + len(arrays)),
        out_specs=out_specs,
        scratch_shapes=[
            pltpu.VMEM((keys, 4 * TOK), F32),
            pltpu.VMEM((keys, 4 * TOK), BF16),
            pltpu.VMEM((DH, keys), BF16),
            pltpu.VMEM((STATS, 4 * TOK), F32),
        ],
        compiler_params=PARAMS,
        cost_estimate=pl.CostEstimate(
            flops=4 * HEADS * keys * 4 * TOK * DH,
            transcendentals=HEADS * keys * 4 * TOK,
            bytes_accessed=12 << 20,
        ),
        name="attend",
    )(where, order, *q, *arrays)


def call(kernel, shape, specs, *arrays):
    return pl.pallas_call(
        kernel,
        out_shape=jax.ShapeDtypeStruct(shape, BF16),
        in_specs=specs,
        out_specs=VM,
        compiler_params=PARAMS,
    )(*arrays)


def share(value, axis):
    wide = jnp.broadcast_to(value[None], (4,) + value.shape)
    return lax.all_to_all(wide, axis, 0, 0, tiled=True)


def local(queries, keys, values, out_weight, block_order):
    together = lax.optimization_barrier
    where = jnp.stack([lax.axis_index(a).astype(jnp.int32) for a in AXES])
    kv = jnp.concatenate([keys, values], axis=0)
    away = swap(kv, "za", 2, 1)
    near0 = share(kv, "zb")
    w = lax.ppermute(out_weight, ("za", "h"), [(0, 0), (1, 2), (2, 1), (3, 3)])[None]
    away, near0, w, queries = together((away, near0, w, queries))

    near1 = share(away, "zb")
    far0 = swap(near0, "c", 2, 1)
    q = [queries] + [swap(queries, "y", 4, j) for j in (1, 2, 3)]
    w = jnp.concatenate([w, swap(w, "za", 2, 1)], axis=0)
    acc, stat = attend(((0, 0), (0, 1)), True, False, where, block_order, q, near0, far0)
    near1, acc, stat, w = together((near1, acc, stat, w))

    far1 = swap(near1, "c", 2, 1)
    w = jnp.concatenate([w, swap(w, "zb", 4, 2)], axis=0)
    acc, stat = attend(((1, 0),), False, False, where, block_order, q, near1, acc, stat)
    part = attend(((1, 1),), False, True, where, block_order, q, far1, acc, stat)
    part, w = together((part, w))

    part = lax.all_to_all(part, "y", 0, 0, tiled=True)
    w = jnp.concatenate([w, swap(w, "zb", 4, 1)], axis=0)
    part, w = together((part, w))

    attended = call(merge_kernel, (TOK, FEAT), [VM], part)
    other = swap(attended, "h", 2, 1)
    own = share(attended, "y")
    w_far = swap(w, "c", 2, 1)
    other, own, w, w_far = together((other, own, w, w_far))

    other = share(other, "y")
    tiles = call(project_kernel, (16, TOK, 256), [SM, VM, VM, VM, VM], where, own, other, w, w_far)
    tiles = lax.all_to_all(tiles, ("x", "y"), 0, 0, tiled=True)
    return call(add_kernel, (TOK, 1024), [VM], tiles)


def solution(mesh):
    fine = Mesh(mesh.devices.reshape(SIZES), AXES)
    in_specs = (P(CTX, HEAD), P(CTX, HEAD), P(CTX, HEAD), P(HEAD, CTX), P())
    return jax.shard_map(local, mesh=fine, in_specs=in_specs, out_specs=P(CTX, HEAD), check_vma=False)
```

```python
import functools
import itertools
import math

import jax
import jax.numpy as jnp
from jax import lax
from jax.experimental import pallas as pl
from jax.experimental.pallas import tpu as pltpu
from jax.sharding import Mesh
from jax.sharding import PartitionSpec as P

AXES = ("za", "zc", "zd", "ya", "yb", "c", "h", "x")
SIZES = (2, 2, 2, 2, 2, 2, 2, 4)
CTX = AXES[:6]
HEAD = AXES[6:]
Y = ("ya", "yb")
TEAM = ("zd", "yb")
DH = 128
TOK = 128
HEADS = 4
FEAT = HEADS * DH
STATS = 16
NEG = -1e30
F32 = jnp.float32
BF16 = jnp.bfloat16


def swap(value, axis):
    return lax.ppermute(value, axis, [(0, 1), (1, 0)])


def attend_kernel(count, near, side, first, last, where, order, *refs):
    q_refs, kv_ref, refs = [ref.at[i] for ref in refs[:2] for i in range(2)], refs[2], refs[3:]
    if not first:
        acc_in, stat_in, *refs = refs
    if last:
        out_ref, *refs = refs
    else:
        acc_out, stat_out, *refs = refs
    score, prob, v_t, parts = refs
    za, zb, y, c = where[0], where[1], where[2], where[3]
    scale = math.log2(math.e) / math.sqrt(DH)
    lane = lax.broadcasted_iota(jnp.int32, (1, TOK), 1)
    row = lax.broadcasted_iota(jnp.int32, (TOK, 1), 0)

    def slot(ctx, index):
        return jnp.where(index < 64, order[2 * ctx], order[2 * ctx + 1]) * 64 + index % 64

    q_pos = jnp.concatenate([slot(((za * 4 + zb) * 4 + (y ^ j)) * 2 + c, lane) for j in range(4)], axis=1)
    blocks = []
    for n in range(count):
        p = n + near
        a, b = za ^ (p & 1), zb ^ (p & 2) ^ (p >> 2)
        v_t[:, n * TOK : (n + 1) * TOK] = kv_ref[n, TOK:, :].T
        blocks.append(slot(((a * 4 + b) * 4 + y) * 2 + (c ^ side), row))
    if last:
        parts[...] = jnp.zeros_like(parts)
    for h in range(HEADS):
        q = jnp.concatenate([ref[:, h * DH : (h + 1) * DH] for ref in q_refs], axis=0)
        top = jnp.full((1, 4 * TOK), NEG, F32) if first else stat_in[h : h + 1, :]
        before = top
        for n, k_pos in enumerate(blocks):
            s = lax.dot_general(kv_ref[n, :TOK, :], q, (((1,), (1,)), ((), ())), preferred_element_type=F32)
            s = jnp.where(k_pos <= q_pos, s * scale, NEG)
            score[n * TOK : (n + 1) * TOK, :] = s
            top = jnp.maximum(top, jnp.max(s, axis=0, keepdims=True))
        total = jnp.zeros((1, 4 * TOK), F32)
        for n in range(len(blocks)):
            e = jnp.exp2(score[n * TOK : (n + 1) * TOK, :] - top)
            total = total + jnp.sum(e, axis=0, keepdims=True)
            prob[n * TOK : (n + 1) * TOK, :] = e.astype(BF16)
        o = jnp.dot(v_t[...], prob[...], preferred_element_type=F32)
        if not first:
            keep = jnp.exp2(before - top)
            total = total + stat_in[HEADS + h : HEADS + h + 1, :] * keep
            o = o + acc_in[h] * keep
        if not last:
            acc_out[h] = o
            stat_out[h : h + 1, :] = top
            stat_out[HEADS + h : HEADS + h + 1, :] = total
            continue
        o = o / total
        for j in range(4):
            out_ref[y ^ j, h * DH : (h + 1) * DH, :] = o[:, j * TOK : (j + 1) * TOK].astype(BF16)
        rest = top + jnp.log2(total)
        for i in range(3):
            part = rest.astype(BF16).astype(F32)
            parts[3 * h + i : 3 * h + i + 1, :] = part
            rest = rest - part
    if last:
        for j in range(4):
            out_ref[y ^ j, FEAT:, :] = parts[:, j * TOK : (j + 1) * TOK].astype(BF16)


def merge_kernel(in_ref, out_ref):
    stats = [in_ref[j, FEAT:, :].astype(F32) for j in range(4)]
    for h in range(HEADS):
        logs = [s[3 * h : 3 * h + 1] + s[3 * h + 1 : 3 * h + 2] + s[3 * h + 2 : 3 * h + 3] for s in stats]
        top = jnp.maximum(jnp.maximum(logs[0], logs[1]), jnp.maximum(logs[2], logs[3]))
        parts = [jnp.exp2(s - top) for s in logs]
        total = parts[0] + parts[1] + parts[2] + parts[3]
        o = jnp.zeros((DH, TOK), F32)
        for j in range(4):
            o = o + in_ref[j, h * DH : (h + 1) * DH, :].astype(F32) * (parts[j] / total)
        out_ref[:, h * DH : (h + 1) * DH] = o.T.astype(BF16)


def copies_kernel(own_ref, other_ref, out_ref):
    for j in range(4):
        out_ref[j, 0] = own_ref[...]
        out_ref[j, 1] = other_ref[...]


def project_kernel(where, pair_ref, near_ref, far_ref, out_ref):
    za, zc, ya, c, h = where[0], where[1] // 2, where[2] // 2, where[3], where[4]
    for r in range(4):
        dest = (zc ^ (r & 1)) * 2 + (ya ^ (r >> 1))
        w = []
        for g in range(2):
            near, far = near_ref[2 * r + g], far_ref[2 * r + g]
            left = jnp.where(c == 0, near, far)
            right = jnp.where(c == 0, far, near)
            w.append(jnp.concatenate([left, right], axis=1))
        w_own = jnp.where(za == h, w[0], w[1])
        w_other = jnp.where(za == h, w[1], w[0])
        for j in range(4):
            acc = jnp.dot(pair_ref[j, 0], w_own, preferred_element_type=F32)
            acc = acc + jnp.dot(pair_ref[j, 1], w_other, preferred_element_type=F32)
            out_ref[j * 4 + dest] = acc.astype(BF16)


def add_kernel(in_ref, out_ref):
    for j in range(4):
        total = in_ref[4 * j].astype(F32)
        for i in range(1, 4):
            total = total + in_ref[4 * j + i].astype(F32)
        out_ref[:, j * 256 : (j + 1) * 256] = total.astype(BF16)


SM = pl.BlockSpec(memory_space=pltpu.SMEM)
VM = pl.BlockSpec(memory_space=pltpu.VMEM)
PARAMS = pltpu.CompilerParams(vmem_limit_bytes=40 << 20)


def attend(near, side, first, last, where, order, q, kv, *arrays):
    count = kv.shape[0]
    keys = count * TOK
    if last:
        out_shape = jax.ShapeDtypeStruct((4, FEAT + STATS, TOK), BF16)
        out_specs = VM
    else:
        out_shape = (
            jax.ShapeDtypeStruct((HEADS, DH, 4 * TOK), F32),
            jax.ShapeDtypeStruct((2 * HEADS, 4 * TOK), F32),
        )
        out_specs = (VM, VM)
    return pl.pallas_call(
        functools.partial(attend_kernel, count, near, side, first, last),
        out_shape=out_shape,
        in_specs=[SM, SM] + [VM] * (3 + len(arrays)),
        out_specs=out_specs,
        scratch_shapes=[
            pltpu.VMEM((keys, 4 * TOK), F32),
            pltpu.VMEM((keys, 4 * TOK), BF16),
            pltpu.VMEM((DH, keys), BF16),
            pltpu.VMEM((STATS, 4 * TOK), F32),
        ],
        compiler_params=PARAMS,
        cost_estimate=pl.CostEstimate(
            flops=4 * HEADS * keys * 4 * TOK * DH,
            transcendentals=HEADS * keys * 4 * TOK,
            bytes_accessed=12 << 20,
        ),
        name="attend",
    )(where, order, *q, kv, *arrays)


def call(kernel, shape, specs, *arrays):
    return pl.pallas_call(
        kernel,
        out_shape=jax.ShapeDtypeStruct(shape, BF16),
        in_specs=specs,
        out_specs=VM,
        compiler_params=PARAMS,
    )(*arrays)


def weight_moves():
    moves = []
    for za, zd, ya, h in itertools.product(range(2), repeat=4):
        source = ((za * 2 + zd) * 2 + ya) * 2 + h
        target = ((h * 2 + ya) * 2 + zd) * 2 + za
        moves.append((source, target))
    return moves


def local(queries, keys, values, out_weight, block_order):
    together = lax.optimization_barrier
    za, zc, zd, ya, yb, c, h, _ = [lax.axis_index(a).astype(jnp.int32) for a in AXES]
    where = jnp.stack([za, zc * 2 + zd, ya * 2 + yb, c, h])
    kv = jnp.concatenate([keys, values], axis=0)[None]
    kv, queries, out_weight = together((kv, queries, out_weight))
    kv_in = swap(kv, "za")
    q = swap(queries, "yb")
    w = lax.ppermute(out_weight, ("za", "zd", "ya", "h"), weight_moves())[None]
    kv_in, q, kv, queries, w = together((kv_in, q, kv, queries, w))

    kv = jnp.concatenate([kv, kv_in], axis=0)
    kv_in = swap(kv, "zc")
    q = jnp.stack([queries, q])
    q_in = swap(q, "ya")
    kv_in, q_in, kv, q, w = together((kv_in, q_in, kv, q, w))

    kv = jnp.concatenate([kv, kv_in], axis=0)
    kv_in = swap(kv, "zd")
    w_in = swap(w, "za")
    q = (q, q_in)
    acc, stat = attend(0, 0, True, False, where, block_order, q, kv)
    kv_in, acc, stat, kv = together((kv_in, acc, stat, kv))

    far = swap(jnp.concatenate([kv, kv_in], axis=0), "c")
    acc, stat = attend(4, 0, False, False, where, block_order, q, kv_in, acc, stat)
    part = attend(0, 1, False, True, where, block_order, q, far, acc, stat)
    part, w, w_in = together((part, w, w_in))

    part = lax.all_to_all(part, Y, 0, 0, tiled=True)
    w = jnp.concatenate([w, w_in], axis=0)
    w_in = swap(w, "zc")
    part, w, w_in = together((part, w, w_in))

    attended = call(merge_kernel, (TOK, FEAT), [VM], part)
    other = swap(attended, "h")
    w = jnp.concatenate([w, w_in], axis=0)
    w_in = swap(w, "ya")
    attended, other, w, w_in = together((attended, other, w, w_in))

    w = jnp.concatenate([w, w_in], axis=0)
    w_far = swap(w, "c")
    pair = call(copies_kernel, (4, 2, TOK, FEAT), [VM, VM], attended, other)
    pair = lax.all_to_all(pair, TEAM, 0, 0, tiled=True)
    tiles = call(project_kernel, (16, TOK, 256), [SM, VM, VM, VM], where, pair, w, w_far)
    tiles = lax.all_to_all(tiles, TEAM + ("x",), 0, 0, tiled=True)
    return call(add_kernel, (TOK, 1024), [VM], tiles)


def solution(mesh):
    fine = Mesh(mesh.devices.reshape(SIZES), AXES)
    in_specs = (P(CTX, HEAD), P(CTX, HEAD), P(CTX, HEAD), P(HEAD, CTX), P())
    return jax.shard_map(local, mesh=fine, in_specs=in_specs, out_specs=P(CTX, HEAD), check_vma=False)
```

```python
import functools
import itertools
import math

import jax
import jax.numpy as jnp
from jax import lax
from jax.experimental import pallas as pl
from jax.experimental.pallas import tpu as pltpu
from jax.sharding import Mesh
from jax.sharding import PartitionSpec as P

AXES = ("za", "zc", "zd", "ya", "yb", "c", "h", "x")
SIZES = (2, 2, 2, 2, 2, 2, 2, 4)
CTX = AXES[:6]
HEAD = AXES[6:]
Y = ("ya", "yb")
TEAM = ("zd", "yb")
DH = 128
TOK = 128
HEADS = 4
FEAT = HEADS * DH
STATS = 16
NEG = -1e30
F32 = jnp.float32
BF16 = jnp.bfloat16


def swap(value, axis):
    return lax.ppermute(value, axis, [(0, 1), (1, 0)])


def attend_kernel(count, near, side, first, last, where, order, *refs):
    q_refs, kv_ref, refs = [ref.at[i] for ref in refs[:2] for i in range(2)], refs[2], refs[3:]
    if not first:
        acc_in, stat_in, *refs = refs
    if last:
        out_ref, *refs = refs
    else:
        acc_out, stat_out, *refs = refs
    score, prob, v_t, parts = refs
    za, zb, y, c = where[0], where[1], where[2], where[3]
    scale = math.log2(math.e) / math.sqrt(DH)
    lane = lax.broadcasted_iota(jnp.int32, (1, TOK), 1)
    row = lax.broadcasted_iota(jnp.int32, (TOK, 1), 0)

    def slot(ctx, index):
        return jnp.where(index < 64, order[2 * ctx], order[2 * ctx + 1]) * 64 + index % 64

    q_pos = jnp.concatenate([slot(((za * 4 + zb) * 4 + (y ^ j)) * 2 + c, lane) for j in range(4)], axis=1)
    blocks = []
    for n in range(count):
        p = n + near
        a, b = za ^ (p & 1), zb ^ (p & 2) ^ (p >> 2)
        v_t[:, n * TOK : (n + 1) * TOK] = kv_ref[n, TOK:, :].T
        blocks.append(slot(((a * 4 + b) * 4 + y) * 2 + (c ^ side), row))
    if last:
        parts[...] = jnp.zeros_like(parts)
    for h in range(HEADS):
        q = jnp.concatenate([ref[:, h * DH : (h + 1) * DH] for ref in q_refs], axis=0)
        top = jnp.full((1, 4 * TOK), NEG, F32) if first else stat_in[h : h + 1, :]
        before = top
        for n, k_pos in enumerate(blocks):
            s = lax.dot_general(kv_ref[n, :TOK, :], q, (((1,), (1,)), ((), ())), preferred_element_type=F32)
            s = jnp.where(k_pos <= q_pos, s * scale, NEG)
            score[n * TOK : (n + 1) * TOK, :] = s
            top = jnp.maximum(top, jnp.max(s, axis=0, keepdims=True))
        total = jnp.zeros((1, 4 * TOK), F32)
        for n in range(len(blocks)):
            e = jnp.exp2(score[n * TOK : (n + 1) * TOK, :] - top)
            total = total + jnp.sum(e, axis=0, keepdims=True)
            prob[n * TOK : (n + 1) * TOK, :] = e.astype(BF16)
        o = jnp.dot(v_t[...], prob[...], preferred_element_type=F32)
        if not first:
            keep = jnp.exp2(before - top)
            total = total + stat_in[HEADS + h : HEADS + h + 1, :] * keep
            o = o + acc_in[h] * keep
        if not last:
            acc_out[h] = o
            stat_out[h : h + 1, :] = top
            stat_out[HEADS + h : HEADS + h + 1, :] = total
            continue
        o = o / total
        for j in range(4):
            out_ref[y ^ j, h * DH : (h + 1) * DH, :] = o[:, j * TOK : (j + 1) * TOK].astype(BF16)
        rest = top + jnp.log2(total)
        for i in range(3):
            part = rest.astype(BF16).astype(F32)
            parts[3 * h + i : 3 * h + i + 1, :] = part
            rest = rest - part
    if last:
        for j in range(4):
            out_ref[y ^ j, FEAT:, :] = parts[:, j * TOK : (j + 1) * TOK].astype(BF16)


def merge_kernel(in_ref, out_ref):
    stats = [in_ref[j, FEAT:, :].astype(F32) for j in range(4)]
    for h in range(HEADS):
        logs = [s[3 * h : 3 * h + 1] + s[3 * h + 1 : 3 * h + 2] + s[3 * h + 2 : 3 * h + 3] for s in stats]
        top = jnp.maximum(jnp.maximum(logs[0], logs[1]), jnp.maximum(logs[2], logs[3]))
        parts = [jnp.exp2(s - top) for s in logs]
        total = parts[0] + parts[1] + parts[2] + parts[3]
        o = jnp.zeros((DH, TOK), F32)
        for j in range(4):
            o = o + in_ref[j, h * DH : (h + 1) * DH, :].astype(F32) * (parts[j] / total)
        out_ref[:, h * DH : (h + 1) * DH] = o.T.astype(BF16)


def stack_kernel(_, *refs):
    out_ref = refs[-1]
    start = 0
    for ref in refs[:-1]:
        out_ref[start : start + ref.shape[0]] = ref[...]
        start += ref.shape[0]


def copies_kernel(own_ref, other_ref, out_ref):
    for j in range(4):
        out_ref[j, 0] = own_ref[...]
        out_ref[j, 1] = other_ref[...]


def project_kernel(where, pair_ref, near_ref, far_ref, out_ref):
    za, zc, ya, c, h = where[0], where[1] // 2, where[2] // 2, where[3], where[4]
    for r in range(4):
        dest = (zc ^ (r & 1)) * 2 + (ya ^ (r >> 1))
        w = []
        for g in range(2):
            near, far = near_ref[2 * r + g], far_ref[2 * r + g]
            left = jnp.where(c == 0, near, far)
            right = jnp.where(c == 0, far, near)
            w.append(jnp.concatenate([left, right], axis=1))
        w_own = jnp.where(za == h, w[0], w[1])
        w_other = jnp.where(za == h, w[1], w[0])
        for j in range(4):
            acc = jnp.dot(pair_ref[j, 0], w_own, preferred_element_type=F32)
            acc = acc + jnp.dot(pair_ref[j, 1], w_other, preferred_element_type=F32)
            out_ref[j * 4 + dest] = acc.astype(BF16)


def add_kernel(in_ref, out_ref):
    for j in range(4):
        total = in_ref[4 * j].astype(F32)
        for i in range(1, 4):
            total = total + in_ref[4 * j + i].astype(F32)
        out_ref[:, j * 256 : (j + 1) * 256] = total.astype(BF16)


SM = pl.BlockSpec(memory_space=pltpu.SMEM)
VM = pl.BlockSpec(memory_space=pltpu.VMEM)
PARAMS = pltpu.CompilerParams(vmem_limit_bytes=40 << 20)


def attend(near, side, first, last, where, order, q, kv, *arrays):
    count = kv.shape[0]
    keys = count * TOK
    if last:
        out_shape = jax.ShapeDtypeStruct((4, FEAT + STATS, TOK), BF16)
        out_specs = VM
    else:
        out_shape = (
            jax.ShapeDtypeStruct((HEADS, DH, 4 * TOK), F32),
            jax.ShapeDtypeStruct((2 * HEADS, 4 * TOK), F32),
        )
        out_specs = (VM, VM)
    return pl.pallas_call(
        functools.partial(attend_kernel, count, near, side, first, last),
        out_shape=out_shape,
        in_specs=[SM, SM] + [VM] * (3 + len(arrays)),
        out_specs=out_specs,
        scratch_shapes=[
            pltpu.VMEM((keys, 4 * TOK), F32),
            pltpu.VMEM((keys, 4 * TOK), BF16),
            pltpu.VMEM((DH, keys), BF16),
            pltpu.VMEM((STATS, 4 * TOK), F32),
        ],
        compiler_params=PARAMS,
        cost_estimate=pl.CostEstimate(
            flops=4 * HEADS * keys * 4 * TOK * DH,
            transcendentals=HEADS * keys * 4 * TOK,
            bytes_accessed=12 << 20,
        ),
        name="attend",
    )(where, order, *q, kv, *arrays)


def call(kernel, shape, specs, *arrays):
    return pl.pallas_call(
        kernel,
        out_shape=jax.ShapeDtypeStruct(shape, BF16),
        in_specs=specs,
        out_specs=VM,
        compiler_params=PARAMS,
    )(*arrays)


COST = pl.CostEstimate(flops=4 << 30, transcendentals=0, bytes_accessed=8 << 20)


def stack(first, *arrays):
    rows = sum(a.shape[0] for a in arrays)
    return pl.pallas_call(
        stack_kernel,
        out_shape=jax.ShapeDtypeStruct((rows,) + arrays[0].shape[1:], BF16),
        in_specs=[pl.BlockSpec(memory_space=pl.ANY)] + [VM] * len(arrays),
        out_specs=VM,
        compiler_params=PARAMS,
        cost_estimate=COST,
    )(first, *arrays)


def weight_moves():
    moves = []
    for za, zd, ya, h in itertools.product(range(2), repeat=4):
        source = ((za * 2 + zd) * 2 + ya) * 2 + h
        target = ((h * 2 + ya) * 2 + zd) * 2 + za
        moves.append((source, target))
    return moves


def local(queries, keys, values, out_weight, block_order):
    together = lax.optimization_barrier
    za, zc, zd, ya, yb, c, h, _ = [lax.axis_index(a).astype(jnp.int32) for a in AXES]
    where = jnp.stack([za, zc * 2 + zd, ya * 2 + yb, c, h])
    kv = jnp.concatenate([keys, values], axis=0)[None]
    kv, queries, out_weight = together((kv, queries, out_weight))
    kv_in = swap(kv, "za")
    q = swap(queries, "yb")
    w = lax.ppermute(out_weight, ("za", "zd", "ya", "h"), weight_moves())[None]
    kv, kv_in, queries, out_weight = together((kv, kv_in, queries, out_weight))

    kv = stack(kv_in, kv, kv_in)
    kv_in = swap(kv, "zc")
    kv, q, queries, w = together((kv, q, queries, w))
    q = jnp.stack([queries, q])
    q_in = swap(q, "ya")
    kv, kv_in = together((kv, kv_in))

    kv = stack(kv_in, kv, kv_in)
    kv, q_in, q = together((kv, q_in, q))
    kv_in = swap(kv, "zd")
    w_in = swap(w, "za")
    q = (q, q_in)
    acc, stat = attend(0, 0, True, False, where, block_order, q, kv)
    kv_in, acc, stat, kv = together((kv_in, acc, stat, kv))

    far = swap(jnp.concatenate([kv, kv_in], axis=0), "c")
    acc, stat = attend(4, 0, False, False, where, block_order, q, kv_in, acc, stat)
    part = attend(0, 1, False, True, where, block_order, q, far, acc, stat)
    part, w, w_in = together((part, w, w_in))

    part = lax.all_to_all(part, Y, 0, 0, tiled=True)
    w = jnp.concatenate([w, w_in], axis=0)
    w_in = swap(w, "zc")
    part, w, w_in = together((part, w, w_in))

    attended = call(merge_kernel, (TOK, FEAT), [VM], part)
    other = swap(attended, "h")
    w = jnp.concatenate([w, w_in], axis=0)
    w_in = swap(w, "ya")
    attended, other, w, w_in = together((attended, other, w, w_in))

    w = jnp.concatenate([w, w_in], axis=0)
    w_far = swap(w, "c")
    pair = call(copies_kernel, (4, 2, TOK, FEAT), [VM, VM], attended, other)
    pair = lax.all_to_all(pair, TEAM, 0, 0, tiled=True)
    tiles = call(project_kernel, (16, TOK, 256), [SM, VM, VM, VM], where, pair, w, w_far)
    tiles = lax.all_to_all(tiles, TEAM + ("x",), 0, 0, tiled=True)
    return call(add_kernel, (TOK, 1024), [VM], tiles)


def solution(mesh):
    fine = Mesh(mesh.devices.reshape(SIZES), AXES)
    in_specs = (P(CTX, HEAD), P(CTX, HEAD), P(CTX, HEAD), P(HEAD, CTX), P())
    return jax.shard_map(local, mesh=fine, in_specs=in_specs, out_specs=P(CTX, HEAD), check_vma=False)
```

```python
import functools
import itertools
import math

import jax
import jax.numpy as jnp
from jax import lax
from jax.experimental import pallas as pl
from jax.experimental.pallas import tpu as pltpu
from jax.sharding import Mesh
from jax.sharding import PartitionSpec as P

AXES = ("za", "zc", "zd", "ya", "yb", "c", "h", "x")
SIZES = (2, 2, 2, 2, 2, 2, 2, 4)
CTX = AXES[:6]
HEAD = AXES[6:]
Y = ("ya", "yb")
TEAM = ("zd", "yb")
DH = 128
TOK = 128
HEADS = 4
FEAT = HEADS * DH
STATS = 16
NEG = -1e30
F32 = jnp.float32
BF16 = jnp.bfloat16


def swap(value, axis):
    return lax.ppermute(value, axis, [(0, 1), (1, 0)])


def attend_kernel(count, near, side, first, last, where, order, *refs):
    q_refs, kv_ref, refs = [ref.at[i] for ref in refs[:2] for i in range(2)], refs[2], refs[3:]
    if not first:
        acc_in, stat_in, *refs = refs
    if last:
        out_ref, *refs = refs
    else:
        acc_out, stat_out, *refs = refs
    score, prob, v_t, parts = refs
    za, zb, y, c = where[0], where[1], where[2], where[3]
    scale = math.log2(math.e) / math.sqrt(DH)
    lane = lax.broadcasted_iota(jnp.int32, (1, TOK), 1)
    row = lax.broadcasted_iota(jnp.int32, (TOK, 1), 0)

    def slot(ctx, index):
        return jnp.where(index < 64, order[2 * ctx], order[2 * ctx + 1]) * 64 + index % 64

    q_pos = jnp.concatenate([slot(((za * 4 + zb) * 4 + (y ^ j)) * 2 + c, lane) for j in range(4)], axis=1)
    blocks = []
    for n in range(count):
        p = n + near
        a, b = za ^ (p & 1), zb ^ (p & 2) ^ (p >> 2)
        v_t[:, n * TOK : (n + 1) * TOK] = kv_ref[n, TOK:, :].T
        blocks.append(slot(((a * 4 + b) * 4 + y) * 2 + (c ^ side), row))
    if last:
        parts[...] = jnp.zeros_like(parts)
    for h in range(HEADS):
        q = jnp.concatenate([ref[:, h * DH : (h + 1) * DH] for ref in q_refs], axis=0)
        top = jnp.full((1, 4 * TOK), NEG, F32) if first else stat_in[h : h + 1, :]
        before = top
        for n, k_pos in enumerate(blocks):
            s = lax.dot_general(kv_ref[n, :TOK, :], q, (((1,), (1,)), ((), ())), preferred_element_type=F32)
            s = jnp.where(k_pos <= q_pos, s * scale, NEG)
            score[n * TOK : (n + 1) * TOK, :] = s
            top = jnp.maximum(top, jnp.max(s, axis=0, keepdims=True))
        total = jnp.zeros((1, 4 * TOK), F32)
        for n in range(len(blocks)):
            e = jnp.exp2(score[n * TOK : (n + 1) * TOK, :] - top)
            total = total + jnp.sum(e, axis=0, keepdims=True)
            prob[n * TOK : (n + 1) * TOK, :] = e.astype(BF16)
        o = jnp.dot(v_t[...], prob[...], preferred_element_type=F32)
        if not first:
            keep = jnp.exp2(before - top)
            total = total + stat_in[HEADS + h : HEADS + h + 1, :] * keep
            o = o + acc_in[h] * keep
        if not last:
            acc_out[h] = o
            stat_out[h : h + 1, :] = top
            stat_out[HEADS + h : HEADS + h + 1, :] = total
            continue
        o = o / total
        for j in range(4):
            out_ref[y ^ j, h * DH : (h + 1) * DH, :] = o[:, j * TOK : (j + 1) * TOK].astype(BF16)
        rest = top + jnp.log2(total)
        for i in range(3):
            part = rest.astype(BF16).astype(F32)
            parts[3 * h + i : 3 * h + i + 1, :] = part
            rest = rest - part
    if last:
        for j in range(4):
            out_ref[y ^ j, FEAT:, :] = parts[:, j * TOK : (j + 1) * TOK].astype(BF16)


def merge_kernel(in_ref, out_ref):
    stats = [in_ref[j, FEAT:, :].astype(F32) for j in range(4)]
    for h in range(HEADS):
        logs = [s[3 * h : 3 * h + 1] + s[3 * h + 1 : 3 * h + 2] + s[3 * h + 2 : 3 * h + 3] for s in stats]
        top = jnp.maximum(jnp.maximum(logs[0], logs[1]), jnp.maximum(logs[2], logs[3]))
        parts = [jnp.exp2(s - top) for s in logs]
        total = parts[0] + parts[1] + parts[2] + parts[3]
        o = jnp.zeros((DH, TOK), F32)
        for j in range(4):
            o = o + in_ref[j, h * DH : (h + 1) * DH, :].astype(F32) * (parts[j] / total)
        out_ref[:, h * DH : (h + 1) * DH] = o.T.astype(BF16)


def stack_kernel(_, *refs):
    out_ref = refs[-1]
    start = 0
    for ref in refs[:-1]:
        out_ref[start : start + ref.shape[0]] = ref[...]
        start += ref.shape[0]


def copies_kernel(own_ref, other_ref, out_ref):
    for j in range(4):
        out_ref[j, 0] = own_ref[...]
        out_ref[j, 1] = other_ref[...]


def project_kernel(where, pair_ref, near_ref, far_ref, out_ref):
    za, zc, ya, c, h = where[0], where[1] // 2, where[2] // 2, where[3], where[4]
    for r in range(4):
        dest = (zc ^ (r & 1)) * 2 + (ya ^ (r >> 1))
        w = []
        for g in range(2):
            near, far = near_ref[2 * r + g], far_ref[2 * r + g]
            left = jnp.where(c == 0, near, far)
            right = jnp.where(c == 0, far, near)
            w.append(jnp.concatenate([left, right], axis=1))
        w_own = jnp.where(za == h, w[0], w[1])
        w_other = jnp.where(za == h, w[1], w[0])
        for j in range(4):
            acc = jnp.dot(pair_ref[j, 0], w_own, preferred_element_type=F32)
            acc = acc + jnp.dot(pair_ref[j, 1], w_other, preferred_element_type=F32)
            out_ref[j * 4 + dest] = acc.astype(BF16)


def add_kernel(in_ref, out_ref):
    for j in range(4):
        total = in_ref[4 * j].astype(F32)
        for i in range(1, 4):
            total = total + in_ref[4 * j + i].astype(F32)
        out_ref[:, j * 256 : (j + 1) * 256] = total.astype(BF16)


SM = pl.BlockSpec(memory_space=pltpu.SMEM)
VM = pl.BlockSpec(memory_space=pltpu.VMEM)
PARAMS = pltpu.CompilerParams(vmem_limit_bytes=40 << 20)


def attend(near, side, first, last, where, order, q, kv, *arrays):
    count = kv.shape[0]
    keys = count * TOK
    if last:
        out_shape = jax.ShapeDtypeStruct((4, FEAT + STATS, TOK), BF16)
        out_specs = VM
    else:
        out_shape = (
            jax.ShapeDtypeStruct((HEADS, DH, 4 * TOK), F32),
            jax.ShapeDtypeStruct((2 * HEADS, 4 * TOK), F32),
        )
        out_specs = (VM, VM)
    return pl.pallas_call(
        functools.partial(attend_kernel, count, near, side, first, last),
        out_shape=out_shape,
        in_specs=[SM, SM] + [VM] * (3 + len(arrays)),
        out_specs=out_specs,
        scratch_shapes=[
            pltpu.VMEM((keys, 4 * TOK), F32),
            pltpu.VMEM((keys, 4 * TOK), BF16),
            pltpu.VMEM((DH, keys), BF16),
            pltpu.VMEM((STATS, 4 * TOK), F32),
        ],
        compiler_params=PARAMS,
        cost_estimate=pl.CostEstimate(
            flops=4 * HEADS * keys * 4 * TOK * DH,
            transcendentals=HEADS * keys * 4 * TOK,
            bytes_accessed=12 << 20,
        ),
        name="attend",
    )(where, order, *q, kv, *arrays)


def call(kernel, shape, specs, *arrays):
    return pl.pallas_call(
        kernel,
        out_shape=jax.ShapeDtypeStruct(shape, BF16),
        in_specs=specs,
        out_specs=VM,
        compiler_params=PARAMS,
    )(*arrays)


COST = pl.CostEstimate(flops=4 << 30, transcendentals=0, bytes_accessed=8 << 20)


def stack(first, *arrays):
    rows = sum(a.shape[0] for a in arrays)
    return pl.pallas_call(
        stack_kernel,
        out_shape=jax.ShapeDtypeStruct((rows,) + arrays[0].shape[1:], BF16),
        in_specs=[pl.BlockSpec(memory_space=pl.ANY)] + [VM] * len(arrays),
        out_specs=VM,
        compiler_params=PARAMS,
        cost_estimate=COST,
    )(first, *arrays)


def weight_moves():
    moves = []
    for za, zd, ya, h in itertools.product(range(2), repeat=4):
        source = ((za * 2 + zd) * 2 + ya) * 2 + h
        target = ((h * 2 + ya) * 2 + zd) * 2 + za
        moves.append((source, target))
    return moves


def local(queries, keys, values, out_weight, block_order):
    together = lax.optimization_barrier
    za, zc, zd, ya, yb, c, h, _ = [lax.axis_index(a).astype(jnp.int32) for a in AXES]
    where = jnp.stack([za, zc * 2 + zd, ya * 2 + yb, c, h])
    kv = jnp.concatenate([keys, values], axis=0)[None]
    kv, queries, out_weight = together((kv, queries, out_weight))
    kv_in = swap(kv, "za")
    q = swap(queries, "yb")
    w = lax.ppermute(out_weight, ("za", "zd", "ya", "h"), weight_moves())[None]
    kv, kv_in, queries, out_weight = together((kv, kv_in, queries, out_weight))

    kv = stack(kv_in, kv, kv_in)
    kv_in = swap(kv, "zc")
    kv, q, queries, w = together((kv, q, queries, w))
    q = jnp.stack([queries, q])
    q_in = swap(q, "ya")
    kv, kv_in = together((kv, kv_in))

    kv = stack(kv_in, kv, kv_in)
    kv, q_in, q = together((kv, q_in, q))
    kv_in = swap(kv, "zd")
    w_in = swap(w, "za")
    q = (q, q_in)
    acc, stat = attend(0, 0, True, False, where, block_order, q, kv)
    kv_in, acc, stat, kv = together((kv_in, acc, stat, kv))

    far = swap(jnp.concatenate([kv, kv_in], axis=0), "c")
    acc, stat = attend(4, 0, False, False, where, block_order, q, kv_in, acc, stat)
    part = attend(0, 1, False, True, where, block_order, q, far, acc, stat)
    part, w, w_in = together((part, w, w_in))

    part = lax.all_to_all(part, Y, 0, 0, tiled=True)
    w = jnp.concatenate([w, w_in], axis=0)
    w_in = swap(w, "zc")
    attended = call(merge_kernel, (TOK, FEAT), [VM], part)
    _, w, w_in = together((attended, w, w_in))
    other = swap(attended, "h")
    w = jnp.concatenate([w, w_in], axis=0)
    w_in = swap(w, "ya")
    pair = pl.pallas_call(
        copies_kernel,
        out_shape=jax.ShapeDtypeStruct((4, 2, TOK, FEAT), BF16),
        in_specs=[VM, VM],
        out_specs=VM,
        compiler_params=PARAMS,
        cost_estimate=COST,
    )(attended, other)
    pair, w, w_in = together((pair, w, w_in))

    w = jnp.concatenate([w, w_in], axis=0)
    w_far = swap(w, "c")
    pair = lax.all_to_all(pair, TEAM, 0, 0, tiled=True)
    tiles = call(project_kernel, (16, TOK, 256), [SM, VM, VM, VM], where, pair, w, w_far)
    tiles = lax.all_to_all(tiles, TEAM + ("x",), 0, 0, tiled=True)
    return call(add_kernel, (TOK, 1024), [VM], tiles)


def solution(mesh):
    fine = Mesh(mesh.devices.reshape(SIZES), AXES)
    in_specs = (P(CTX, HEAD), P(CTX, HEAD), P(CTX, HEAD), P(HEAD, CTX), P())
    return jax.shard_map(local, mesh=fine, in_specs=in_specs, out_specs=P(CTX, HEAD), check_vma=False)
```

```python
import functools
import itertools
import math

import jax
import jax.numpy as jnp
from jax import lax
from jax.experimental import pallas as pl
from jax.experimental.pallas import tpu as pltpu
from jax.sharding import Mesh
from jax.sharding import PartitionSpec as P

AXES = ("za", "zc", "zd", "ya", "yb", "c", "h", "x")
SIZES = (2, 2, 2, 2, 2, 2, 2, 4)
CTX = AXES[:6]
HEAD = AXES[6:]
Y = ("ya", "yb")
TEAM = ("zd", "yb")
DH = 128
TOK = 128
HEADS = 4
FEAT = HEADS * DH
STATS = 16
NEG = -1e30
F32 = jnp.float32
BF16 = jnp.bfloat16


def swap(value, axis):
    return lax.ppermute(value, axis, [(0, 1), (1, 0)])


def attend_kernel(count, near, side, first, last, where, order, *refs):
    q_refs, kv_ref, refs = [ref.at[i] for ref in refs[:2] for i in range(2)], refs[2], refs[3:]
    if not first:
        acc_in, stat_in, *refs = refs
    if last:
        out_ref, *refs = refs
    else:
        acc_out, stat_out, *refs = refs
    score, prob, v_t, parts = refs
    za, zb, y, c = where[0], where[1], where[2], where[3]
    scale = math.log2(math.e) / math.sqrt(DH)
    lane = lax.broadcasted_iota(jnp.int32, (1, TOK), 1)
    row = lax.broadcasted_iota(jnp.int32, (TOK, 1), 0)

    def slot(ctx, index):
        return jnp.where(index < 64, order[2 * ctx], order[2 * ctx + 1]) * 64 + index % 64

    q_pos = jnp.concatenate([slot(((za * 4 + zb) * 4 + (y ^ j)) * 2 + c, lane) for j in range(4)], axis=1)
    blocks = []
    for n in range(count):
        p = n + near
        a, b = za ^ (p & 1), zb ^ (p & 2) ^ (p >> 2)
        v_t[:, n * TOK : (n + 1) * TOK] = kv_ref[n, TOK:, :].T
        blocks.append(slot(((a * 4 + b) * 4 + y) * 2 + (c ^ side), row))
    if last:
        parts[...] = jnp.zeros_like(parts)
    for h in range(HEADS):
        q = jnp.concatenate([ref[:, h * DH : (h + 1) * DH] for ref in q_refs], axis=0)
        top = jnp.full((1, 4 * TOK), NEG, F32) if first else stat_in[h : h + 1, :]
        before = top
        for n, k_pos in enumerate(blocks):
            s = lax.dot_general(kv_ref[n, :TOK, :], q, (((1,), (1,)), ((), ())), preferred_element_type=F32)
            s = jnp.where(k_pos <= q_pos, s * scale, NEG)
            score[n * TOK : (n + 1) * TOK, :] = s
            top = jnp.maximum(top, jnp.max(s, axis=0, keepdims=True))
        total = jnp.zeros((1, 4 * TOK), F32)
        for n in range(len(blocks)):
            e = jnp.exp2(score[n * TOK : (n + 1) * TOK, :] - top)
            total = total + jnp.sum(e, axis=0, keepdims=True)
            prob[n * TOK : (n + 1) * TOK, :] = e.astype(BF16)
        o = jnp.dot(v_t[...], prob[...], preferred_element_type=F32)
        if not first:
            keep = jnp.exp2(before - top)
            total = total + stat_in[HEADS + h : HEADS + h + 1, :] * keep
            o = o + acc_in[h] * keep
        if not last:
            acc_out[h] = o
            stat_out[h : h + 1, :] = top
            stat_out[HEADS + h : HEADS + h + 1, :] = total
            continue
        o = o / total
        for j in range(4):
            out_ref[y ^ j, h * DH : (h + 1) * DH, :] = o[:, j * TOK : (j + 1) * TOK].astype(BF16)
        rest = top + jnp.log2(total)
        for i in range(3):
            part = rest.astype(BF16).astype(F32)
            parts[3 * h + i : 3 * h + i + 1, :] = part
            rest = rest - part
    if last:
        for j in range(4):
            out_ref[y ^ j, FEAT:, :] = parts[:, j * TOK : (j + 1) * TOK].astype(BF16)


def merge_kernel(in_ref, out_ref):
    stats = [in_ref[j, FEAT:, :].astype(F32) for j in range(4)]
    for h in range(HEADS):
        logs = [s[3 * h : 3 * h + 1] + s[3 * h + 1 : 3 * h + 2] + s[3 * h + 2 : 3 * h + 3] for s in stats]
        top = jnp.maximum(jnp.maximum(logs[0], logs[1]), jnp.maximum(logs[2], logs[3]))
        parts = [jnp.exp2(s - top) for s in logs]
        total = parts[0] + parts[1] + parts[2] + parts[3]
        o = jnp.zeros((DH, TOK), F32)
        for j in range(4):
            o = o + in_ref[j, h * DH : (h + 1) * DH, :].astype(F32) * (parts[j] / total)
        out_ref[:, h * DH : (h + 1) * DH] = o.T.astype(BF16)


def stack_kernel(_, *refs):
    out_ref = refs[-1]
    start = 0
    for ref in refs[:-1]:
        out_ref[start : start + ref.shape[0]] = ref[...]
        start += ref.shape[0]


def copies_kernel(own_ref, other_ref, out_ref):
    for j in range(4):
        out_ref[j, 0] = own_ref[...]
        out_ref[j, 1] = other_ref[...]


def project_kernel(where, pair_ref, near_ref, far_ref, out_ref):
    za, zc, ya, c, h = where[0], where[1] // 2, where[2] // 2, where[3], where[4]
    for r in range(4):
        dest = (zc ^ (r & 1)) * 2 + (ya ^ (r >> 1))
        w = []
        for g in range(2):
            near, far = near_ref[2 * r + g], far_ref[2 * r + g]
            left = jnp.where(c == 0, near, far)
            right = jnp.where(c == 0, far, near)
            w.append(jnp.concatenate([left, right], axis=1))
        w_own = jnp.where(za == h, w[0], w[1])
        w_other = jnp.where(za == h, w[1], w[0])
        for j in range(4):
            acc = jnp.dot(pair_ref[j, 0], w_own, preferred_element_type=F32)
            acc = acc + jnp.dot(pair_ref[j, 1], w_other, preferred_element_type=F32)
            out_ref[j * 4 + dest] = acc.astype(BF16)


def add_kernel(in_ref, out_ref):
    for j in range(4):
        total = in_ref[4 * j].astype(F32)
        for i in range(1, 4):
            total = total + in_ref[4 * j + i].astype(F32)
        out_ref[:, j * 256 : (j + 1) * 256] = total.astype(BF16)


SM = pl.BlockSpec(memory_space=pltpu.SMEM)
VM = pl.BlockSpec(memory_space=pltpu.VMEM)
PARAMS = pltpu.CompilerParams(vmem_limit_bytes=40 << 20)


def attend(near, side, first, last, where, order, q, kv, *arrays):
    count = kv.shape[0]
    keys = count * TOK
    if last:
        out_shape = jax.ShapeDtypeStruct((4, FEAT + STATS, TOK), BF16)
        out_specs = VM
    else:
        out_shape = (
            jax.ShapeDtypeStruct((HEADS, DH, 4 * TOK), F32),
            jax.ShapeDtypeStruct((2 * HEADS, 4 * TOK), F32),
        )
        out_specs = (VM, VM)
    return pl.pallas_call(
        functools.partial(attend_kernel, count, near, side, first, last),
        out_shape=out_shape,
        in_specs=[SM, SM] + [VM] * (3 + len(arrays)),
        out_specs=out_specs,
        scratch_shapes=[
            pltpu.VMEM((keys, 4 * TOK), F32),
            pltpu.VMEM((keys, 4 * TOK), BF16),
            pltpu.VMEM((DH, keys), BF16),
            pltpu.VMEM((STATS, 4 * TOK), F32),
        ],
        compiler_params=PARAMS,
        cost_estimate=pl.CostEstimate(
            flops=4 * HEADS * keys * 4 * TOK * DH,
            transcendentals=HEADS * keys * 4 * TOK,
            bytes_accessed=12 << 20,
        ),
        name="attend",
    )(where, order, *q, kv, *arrays)


def call(kernel, shape, specs, *arrays):
    return pl.pallas_call(
        kernel,
        out_shape=jax.ShapeDtypeStruct(shape, BF16),
        in_specs=specs,
        out_specs=VM,
        compiler_params=PARAMS,
    )(*arrays)


COST = pl.CostEstimate(flops=4 << 30, transcendentals=0, bytes_accessed=8 << 20)


def stack(first, *arrays):
    rows = sum(a.shape[0] for a in arrays)
    return pl.pallas_call(
        stack_kernel,
        out_shape=jax.ShapeDtypeStruct((rows,) + arrays[0].shape[1:], BF16),
        in_specs=[pl.BlockSpec(memory_space=pl.ANY)] + [VM] * len(arrays),
        out_specs=VM,
        compiler_params=PARAMS,
        cost_estimate=COST,
    )(first, *arrays)


def weight_moves():
    moves = []
    for za, zd, ya, h in itertools.product(range(2), repeat=4):
        source = ((za * 2 + zd) * 2 + ya) * 2 + h
        target = ((h * 2 + ya) * 2 + zd) * 2 + za
        moves.append((source, target))
    return moves


def local(queries, keys, values, out_weight, block_order):
    together = lax.optimization_barrier
    za, zc, zd, ya, yb, c, h, _ = [lax.axis_index(a).astype(jnp.int32) for a in AXES]
    where = jnp.stack([za, zc * 2 + zd, ya * 2 + yb, c, h])
    kv = jnp.concatenate([keys, values], axis=0)[None]
    kv, queries, out_weight = together((kv, queries, out_weight))
    kv_in = swap(kv, "za")
    q = swap(queries, "yb")
    w = lax.ppermute(out_weight, ("za", "zd", "ya", "h"), weight_moves())[None]
    kv, kv_in, queries, out_weight = together((kv, kv_in, queries, out_weight))

    kv = stack(kv_in, kv, kv_in)
    kv_in = swap(kv, "zc")
    kv, q, queries, w = together((kv, q, queries, w))
    q = jnp.stack([queries, q])
    q_in = swap(q, "ya")
    kv, kv_in = together((kv, kv_in))

    kv = stack(kv_in, kv, kv_in)
    kv, q_in, q = together((kv, q_in, q))
    kv_in = swap(kv, "zd")
    w_in = swap(w, "za")
    q = (q, q_in)
    acc, stat = attend(0, 0, True, False, where, block_order, q, kv)
    kv_in, acc, stat, kv = together((kv_in, acc, stat, kv))

    far = swap(jnp.concatenate([kv, kv_in], axis=0), "c")
    acc, stat = attend(4, 0, False, False, where, block_order, q, kv_in, acc, stat)
    part = attend(0, 1, False, True, where, block_order, q, far, acc, stat)
    _, w, w_in = together((part, w, w_in))

    part = lax.all_to_all(part, Y, 0, 0, tiled=True)
    w = jnp.concatenate([w, w_in], axis=0)
    w_in = swap(w, "zc")
    attended = call(merge_kernel, (TOK, FEAT), [VM], part)
    _, w, w_in = together((attended, w, w_in))
    other = swap(attended, "h")
    w = jnp.concatenate([w, w_in], axis=0)
    w_in = swap(w, "ya")
    pair = pl.pallas_call(
        copies_kernel,
        out_shape=jax.ShapeDtypeStruct((4, 2, TOK, FEAT), BF16),
        in_specs=[VM, VM],
        out_specs=VM,
        compiler_params=PARAMS,
        cost_estimate=COST,
    )(attended, other)
    pair, w, w_in = together((pair, w, w_in))

    w = jnp.concatenate([w, w_in], axis=0)
    w_far = swap(w, "c")
    pair = lax.all_to_all(pair, TEAM, 0, 0, tiled=True)
    tiles = call(project_kernel, (16, TOK, 256), [SM, VM, VM, VM], where, pair, w, w_far)
    tiles = lax.all_to_all(tiles, TEAM + ("x",), 0, 0, tiled=True)
    return call(add_kernel, (TOK, 1024), [VM], tiles)


def solution(mesh):
    fine = Mesh(mesh.devices.reshape(SIZES), AXES)
    in_specs = (P(CTX, HEAD), P(CTX, HEAD), P(CTX, HEAD), P(HEAD, CTX), P())
    return jax.shard_map(local, mesh=fine, in_specs=in_specs, out_specs=P(CTX, HEAD), check_vma=False)
```

```python
import functools
import itertools
import math

import jax
import jax.numpy as jnp
from jax import lax
from jax.experimental import pallas as pl
from jax.experimental.pallas import tpu as pltpu
from jax.sharding import Mesh
from jax.sharding import PartitionSpec as P

AXES = ("za", "zc", "zd", "ya", "yb", "c", "h", "x")
SIZES = (2, 2, 2, 2, 2, 2, 2, 4)
CTX = AXES[:6]
HEAD = AXES[6:]
Y = ("ya", "yb")
TEAM = ("zd", "yb")
DH = 128
TOK = 128
HEADS = 4
FEAT = HEADS * DH
STATS = 16
NEG = -1e30
F32 = jnp.float32
BF16 = jnp.bfloat16


def swap(value, axis):
    return lax.ppermute(value, axis, [(0, 1), (1, 0)])


def attend_kernel(count, near, side, first, last, where, order, *refs):
    q_refs, kv_ref, refs = [ref.at[i] for ref in refs[:2] for i in range(2)], refs[2], refs[3:]
    if not first:
        acc_in, stat_in, *refs = refs
    if last:
        out_ref, *refs = refs
    else:
        acc_out, stat_out, *refs = refs
    score, prob, v_t, parts = refs
    za, zb, y, c = where[0], where[1], where[2], where[3]
    scale = math.log2(math.e) / math.sqrt(DH)
    lane = lax.broadcasted_iota(jnp.int32, (1, TOK), 1)
    row = lax.broadcasted_iota(jnp.int32, (TOK, 1), 0)

    def slot(ctx, index):
        return jnp.where(index < 64, order[2 * ctx], order[2 * ctx + 1]) * 64 + index % 64

    q_pos = jnp.concatenate([slot(((za * 4 + zb) * 4 + (y ^ j)) * 2 + c, lane) for j in range(4)], axis=1)
    blocks = []
    for n in range(count):
        p = n + near
        a, b = za ^ (p & 1), zb ^ (p & 2) ^ (p >> 2)
        v_t[:, n * TOK : (n + 1) * TOK] = kv_ref[n, TOK:, :].T
        blocks.append(slot(((a * 4 + b) * 4 + y) * 2 + (c ^ side), row))
    if last:
        parts[...] = jnp.zeros_like(parts)
    for h in range(HEADS):
        q = jnp.concatenate([ref[:, h * DH : (h + 1) * DH] for ref in q_refs], axis=0)
        top = jnp.full((1, 4 * TOK), NEG, F32) if first else stat_in[h : h + 1, :]
        before = top
        for n, k_pos in enumerate(blocks):
            s = lax.dot_general(kv_ref[n, :TOK, :], q, (((1,), (1,)), ((), ())), preferred_element_type=F32)
            s = jnp.where(k_pos <= q_pos, s * scale, NEG)
            score[n * TOK : (n + 1) * TOK, :] = s
            top = jnp.maximum(top, jnp.max(s, axis=0, keepdims=True))
        total = jnp.zeros((1, 4 * TOK), F32)
        for n in range(len(blocks)):
            e = jnp.exp2(score[n * TOK : (n + 1) * TOK, :] - top)
            total = total + jnp.sum(e, axis=0, keepdims=True)
            prob[n * TOK : (n + 1) * TOK, :] = e.astype(BF16)
        o = jnp.dot(v_t[...], prob[...], preferred_element_type=F32)
        if not first:
            keep = jnp.exp2(before - top)
            total = total + stat_in[HEADS + h : HEADS + h + 1, :] * keep
            o = o + acc_in[h] * keep
        if not last:
            acc_out[h] = o
            stat_out[h : h + 1, :] = top
            stat_out[HEADS + h : HEADS + h + 1, :] = total
            continue
        o = o / total
        for j in range(4):
            out_ref[y ^ j, h * DH : (h + 1) * DH, :] = o[:, j * TOK : (j + 1) * TOK].astype(BF16)
        rest = top + jnp.log2(total)
        for i in range(3):
            part = rest.astype(BF16).astype(F32)
            parts[3 * h + i : 3 * h + i + 1, :] = part
            rest = rest - part
    if last:
        for j in range(4):
            out_ref[y ^ j, FEAT:, :] = parts[:, j * TOK : (j + 1) * TOK].astype(BF16)


def merge_kernel(in_ref, out_ref):
    stats = [in_ref[j, FEAT:, :].astype(F32) for j in range(4)]
    for h in range(HEADS):
        logs = [s[3 * h : 3 * h + 1] + s[3 * h + 1 : 3 * h + 2] + s[3 * h + 2 : 3 * h + 3] for s in stats]
        top = jnp.maximum(jnp.maximum(logs[0], logs[1]), jnp.maximum(logs[2], logs[3]))
        parts = [jnp.exp2(s - top) for s in logs]
        total = parts[0] + parts[1] + parts[2] + parts[3]
        o = jnp.zeros((DH, TOK), F32)
        for j in range(4):
            o = o + in_ref[j, h * DH : (h + 1) * DH, :].astype(F32) * (parts[j] / total)
        out_ref[:, h * DH : (h + 1) * DH] = o.T.astype(BF16)


def stack_kernel(_, *refs):
    out_ref = refs[-1]
    start = 0
    for ref in refs[:-1]:
        out_ref[start : start + ref.shape[0]] = ref[...]
        start += ref.shape[0]


def copies_kernel(own_ref, other_ref, out_ref):
    for j in range(4):
        out_ref[j, 0] = own_ref[...]
        out_ref[j, 1] = other_ref[...]


def project_kernel(where, pair_ref, near_ref, far_ref, out_ref):
    za, zc, ya, c, h = where[0], where[1] // 2, where[2] // 2, where[3], where[4]
    for r in range(4):
        dest = (zc ^ (r & 1)) * 2 + (ya ^ (r >> 1))
        w = []
        for g in range(2):
            near, far = near_ref[2 * r + g], far_ref[2 * r + g]
            left = jnp.where(c == 0, near, far)
            right = jnp.where(c == 0, far, near)
            w.append(jnp.concatenate([left, right], axis=1))
        w_own = jnp.where(za == h, w[0], w[1])
        w_other = jnp.where(za == h, w[1], w[0])
        for j in range(4):
            acc = jnp.dot(pair_ref[j, 0], w_own, preferred_element_type=F32)
            acc = acc + jnp.dot(pair_ref[j, 1], w_other, preferred_element_type=F32)
            out_ref[j * 4 + dest] = acc.astype(BF16)


def add_kernel(in_ref, out_ref):
    for j in range(4):
        total = in_ref[4 * j].astype(F32)
        for i in range(1, 4):
            total = total + in_ref[4 * j + i].astype(F32)
        out_ref[:, j * 256 : (j + 1) * 256] = total.astype(BF16)


SM = pl.BlockSpec(memory_space=pltpu.SMEM)
VM = pl.BlockSpec(memory_space=pltpu.VMEM)
PARAMS = pltpu.CompilerParams(vmem_limit_bytes=40 << 20)


def attend(near, side, first, last, where, order, q, kv, *arrays):
    count = kv.shape[0]
    keys = count * TOK
    if last:
        out_shape = jax.ShapeDtypeStruct((4, FEAT + STATS, TOK), BF16)
        out_specs = VM
    else:
        out_shape = (
            jax.ShapeDtypeStruct((HEADS, DH, 4 * TOK), F32),
            jax.ShapeDtypeStruct((2 * HEADS, 4 * TOK), F32),
        )
        out_specs = (VM, VM)
    return pl.pallas_call(
        functools.partial(attend_kernel, count, near, side, first, last),
        out_shape=out_shape,
        in_specs=[SM, SM] + [VM] * (3 + len(arrays)),
        out_specs=out_specs,
        scratch_shapes=[
            pltpu.VMEM((keys, 4 * TOK), F32),
            pltpu.VMEM((keys, 4 * TOK), BF16),
            pltpu.VMEM((DH, keys), BF16),
            pltpu.VMEM((STATS, 4 * TOK), F32),
        ],
        compiler_params=PARAMS,
        cost_estimate=pl.CostEstimate(
            flops=4 * HEADS * keys * 4 * TOK * DH,
            transcendentals=HEADS * keys * 4 * TOK,
            bytes_accessed=12 << 20,
        ),
        name="attend",
    )(where, order, *q, kv, *arrays)


def call(kernel, shape, specs, *arrays):
    return pl.pallas_call(
        kernel,
        out_shape=jax.ShapeDtypeStruct(shape, BF16),
        in_specs=specs,
        out_specs=VM,
        compiler_params=PARAMS,
    )(*arrays)


COST = pl.CostEstimate(flops=4 << 30, transcendentals=0, bytes_accessed=8 << 20)


def stack(first, *arrays):
    rows = sum(a.shape[0] for a in arrays)
    return pl.pallas_call(
        stack_kernel,
        out_shape=jax.ShapeDtypeStruct((rows,) + arrays[0].shape[1:], BF16),
        in_specs=[pl.BlockSpec(memory_space=pl.ANY)] + [VM] * len(arrays),
        out_specs=VM,
        compiler_params=PARAMS,
        cost_estimate=COST,
    )(first, *arrays)


def weight_moves():
    moves = []
    for za, zd, ya, h in itertools.product(range(2), repeat=4):
        source = ((za * 2 + zd) * 2 + ya) * 2 + h
        target = ((h * 2 + ya) * 2 + zd) * 2 + za
        moves.append((source, target))
    return moves


def local(queries, keys, values, out_weight, block_order):
    together = lax.optimization_barrier
    za, zc, zd, ya, yb, c, h, _ = [lax.axis_index(a).astype(jnp.int32) for a in AXES]
    where = jnp.stack([za, zc * 2 + zd, ya * 2 + yb, c, h])
    kv = jnp.concatenate([keys, values], axis=0)[None]
    kv, queries, out_weight = together((kv, queries, out_weight))
    kv_in = swap(kv, "za")
    q = swap(queries, "yb")
    w = lax.ppermute(out_weight, ("za", "zd", "ya", "h"), weight_moves())[None]
    kv, kv_in, queries, out_weight = together((kv, kv_in, queries, out_weight))

    kv = stack(kv_in, kv, kv_in)
    kv_in = swap(kv, "zc")
    kv, q, queries, w = together((kv, q, queries, w))
    q = jnp.stack([queries, q])
    q_in = swap(q, "ya")
    kv, kv_in = together((kv, kv_in))

    kv = stack(kv_in, kv, kv_in)
    kv, q_in, q = together((kv, q_in, q))
    kv_in = swap(kv, "zd")
    w_in = swap(w, "za")
    q = (q, q_in)
    acc, stat = attend(0, 0, True, False, where, block_order, q, kv)
    kv_in, acc, stat, kv = together((kv_in, acc, stat, kv))

    far = swap(jnp.concatenate([kv, kv_in], axis=0), "c")
    acc, stat = attend(4, 0, False, False, where, block_order, q, kv_in, acc, stat)
    part = attend(0, 1, False, True, where, block_order, q, far, acc, stat)
    _, w, w_in = together((part, w, w_in))

    part = lax.all_to_all(part, Y, 0, 0, tiled=True)
    w = jnp.concatenate([w, w_in], axis=0)
    w_in = swap(w, "zc")
    attended = call(merge_kernel, (TOK, FEAT), [VM], part)
    _, w, w_in = together((attended, w, w_in))
    other = swap(attended, "h")
    w = jnp.concatenate([w, w_in], axis=0)
    w_in = swap(w, "ya")
    pair = pl.pallas_call(
        copies_kernel,
        out_shape=jax.ShapeDtypeStruct((4, 2, TOK, FEAT), BF16),
        in_specs=[VM, VM],
        out_specs=VM,
        compiler_params=PARAMS,
        cost_estimate=COST,
    )(attended, other)
    _, w, w_in = together((pair, w, w_in))

    w = jnp.concatenate([w, w_in], axis=0)
    w_far = swap(w, "c")
    pair = lax.all_to_all(pair, TEAM, 0, 0, tiled=True)
    tiles = call(project_kernel, (16, TOK, 256), [SM, VM, VM, VM], where, pair, w, w_far)
    tiles = lax.all_to_all(tiles, TEAM + ("x",), 0, 0, tiled=True)
    return call(add_kernel, (TOK, 1024), [VM], tiles)


def solution(mesh):
    fine = Mesh(mesh.devices.reshape(SIZES), AXES)
    in_specs = (P(CTX, HEAD), P(CTX, HEAD), P(CTX, HEAD), P(HEAD, CTX), P())
    return jax.shard_map(local, mesh=fine, in_specs=in_specs, out_specs=P(CTX, HEAD), check_vma=False)
```
